32 devices in a mesh: seq: 4 (over y, x), head: 8 (over z, core).
Axes of the slice: x: 2, y: 2, z: 4, core: 2. Of those that a mesh axis runs over, the one named last changes fastest.
Arguments:
- inputs: bfloat16 [4096, 6144], P('seq', 'head'), may hold values from -6 to 6
- projection: bfloat16 [6144, 3, 4096], P('seq', None, 'head'), may hold values from -0.078125 to 0.078125
- cotangent: bfloat16 [4096, 4096], P('seq', 'head'), may hold values from -0.3125 to 0.3125
- log_decay: float32 [32, 4096], P('head', 'seq'), may hold values from -0.7 to 0
- document_starts: int32 [4], replicated, may hold values from 0 to 3328, as said below
Outputs:
- input_gradient: bfloat16 [4096, 6144], P('seq', 'head')
- weight_gradient: bfloat16 [6144, 3, 4096], P('seq', None, 'head')
The draws below stay inside these ranges and needn't reach their ends.
Inputs may be any that keep to these rules, and one draw needn't show every extreme that they name: `document_starts`: strictly increasing; the first is 0 and the last is (3) * 1024 + 256.
All inputs are finite; a program needn't handle non-finite values.
Results may differ from the reference program's by a relative error of at most 0.02.
Values may be sent and summed in bfloat16 or wider, within the bound.
A program may use at most 192 MiB of HBM per device.

```python
import jax
import jax.numpy as jnp
from jax import lax

D = 6144
LOCAL_HEADS = 32
HEAD_DIM = 128
BLOCK = 256
TOK_DEV = 1024
PACKED_TOKENS = 4096
NDOC = 4
N_SEQ = 4
N_HEAD = 8


def draw_log_decay(key, part):
    parallel_flows = jax.random.split(jax.random.fold_in(key, 11), 7)
    strong_share = 0.5
    strong = jax.random.uniform(parallel_flows[0], (LOCAL_HEADS, 1, 1)) < strong_share
    fast_rate = jnp.exp(jax.random.uniform(parallel_flows[1], (LOCAL_HEADS, 1, 1), jnp.float32, jnp.log(1.0 / 50.0), jnp.log(1.0 / 30.0)))
    slow_rate = jnp.exp(jax.random.uniform(parallel_flows[2], (LOCAL_HEADS, 1, 1), jnp.float32, jnp.log(0.05), jnp.log(0.4))) / PACKED_TOKENS
    rate = jnp.where(strong, fast_rate, slow_rate)
    blocks = PACKED_TOKENS // BLOCK
    block_factor = jnp.exp(jax.random.uniform(parallel_flows[3], (LOCAL_HEADS, blocks, 1), jnp.float32, jnp.log(0.5), jnp.log(2.0)))
    jitter = jax.random.uniform(parallel_flows[4], (LOCAL_HEADS, blocks, BLOCK), jnp.float32, 0.5, 2.0)
    constant_level = -(rate * block_factor * jitter).reshape(LOCAL_HEADS, PACKED_TOKENS)
    sudden_spike = jax.random.uniform(parallel_flows[5], (LOCAL_HEADS, PACKED_TOKENS)) < 3.0 / PACKED_TOKENS
    nesting_level = jnp.log(jax.random.uniform(parallel_flows[6], (LOCAL_HEADS, PACKED_TOKENS), jnp.float32, 0.5, 0.8))
    return jnp.where(sudden_spike, nesting_level, constant_level).astype(jnp.float32)


def draw_document_starts(key, part):
    parallel_flows = jax.random.split(jax.random.fold_in(key, 23), 2)
    span = PACKED_TOKENS // NDOC
    jitter = span // 4
    offsets = jax.random.randint(parallel_flows[0], (NDOC,), -jitter, jitter + 1)
    aligned_flag = jax.random.randint(parallel_flows[1], (NDOC,), 0, 2)
    order = jnp.arange(NDOC, dtype=jnp.int32)
    base = order * span + offsets
    aligned = base // BLOCK * BLOCK
    starts = jnp.where(aligned_flag == 1, aligned, base)
    starts = jnp.where(order == 0, 0, starts)
    starts = jnp.where(order == NDOC - 1, (NDOC - 1) * span + jitter, starts)
    return starts.astype(jnp.int32)


def block_scale(own_key, shape, cuts, low, largest):
    loudness, own = 1.0, jax.random.fold_in(own_key, 6)
    for dim, blocks in cuts:
        heights = jnp.exp(jax.random.uniform(jax.random.fold_in(own, dim), (blocks,), jnp.float32, low / len(cuts), largest / len(cuts)))
        loudness = loudness * jnp.repeat(heights, shape[dim] // blocks).reshape([-1 if axis == dim else 1 for axis in range(len(shape))])
    return loudness


def normal_values(rng, dims, deviation, most, shards=(), kind=jnp.bfloat16):
    entries = deviation * jax.random.normal(rng, dims, jnp.float32)
    if shards:
        entries = entries * block_scale(rng, dims, shards, -0.22, 0.18)
    return jnp.clip(entries, -most, most).astype(kind)


def setup_inputs(seed: int = 0) -> dict:
    seeds = jax.random.split(jax.random.key(seed), 6)
    return {
        "inputs": normal_values(seeds[0], (PACKED_TOKENS, D), 1.0, 6.0, ((0, 4), (1, 8))),
        "projection": normal_values(seeds[1], (D, 3, LOCAL_HEADS * HEAD_DIM), D ** -0.5, 0.078125, ((0, 4), (2, 8))),
        "cotangent": normal_values(seeds[2], (PACKED_TOKENS, LOCAL_HEADS * HEAD_DIM), 0.05, 0.3125, ((0, 4), (1, 8))),
        "log_decay": draw_log_decay(jax.random.fold_in(seeds[5], 71), 0),
        "document_starts": draw_document_starts(jax.random.fold_in(seeds[5], 71), 0),
    }


def silu_slope(point):
    sigma = jax.nn.sigmoid(point)
    return sigma * (1.0 + point * (1.0 - sigma))


def block_factors(decay_sum, doc_index, doc_begin):
    inside = jnp.arange(doc_index.shape[-1], dtype=jnp.int32)
    causal = inside[:, None] >= inside[None, :]
    same_doc = (doc_index[:, :, None] == doc_index[:, None, :]) & causal[None]
    spread = jnp.minimum(decay_sum[..., :, None] - decay_sum[..., None, :], 0.0)
    pair_weight = jnp.where(same_doc[None], jnp.exp(spread), 0.0)
    to_end = jnp.where((doc_index == doc_index[:, -1:])[None], jnp.exp(decay_sum[..., -1:] - decay_sum), 0.0)
    began_flag = doc_index == (doc_index[:, :1] - doc_begin[:, :1].astype(jnp.int32))
    from_start = jnp.where(began_flag[None], jnp.exp(decay_sum), 0.0)
    return pair_weight, to_end, from_start, from_start[..., -1]


def reference(inputs, projection, cotangent, log_decay, document_starts):
    columns = LOCAL_HEADS * HEAD_DIM
    blocks = PACKED_TOKENS // BLOCK
    query_scale = HEAD_DIM ** -0.5
    flat_weight = projection.reshape(D, 3 * columns)
    projected = jnp.dot(inputs, flat_weight, preferred_element_type=jnp.float32).reshape(PACKED_TOKENS, 3, columns)
    queries = (jax.nn.silu(projected[:, 0]) * query_scale).astype(jnp.bfloat16)
    keys = jax.nn.silu(projected[:, 1]).astype(jnp.bfloat16)
    values = projected[:, 2].astype(jnp.bfloat16)

    def split_blocks(table):
        return table.reshape(blocks, BLOCK, LOCAL_HEADS, HEAD_DIM).transpose(2, 0, 1, 3).astype(jnp.float32)

    def merge_blocks(table):
        return table.transpose(1, 2, 0, 3).reshape(PACKED_TOKENS, columns)

    queries_b = split_blocks(queries)
    keys_b = split_blocks(keys)
    values_b = split_blocks(values)
    upstream = split_blocks(cotangent)
    positions = jnp.arange(PACKED_TOKENS, dtype=jnp.int32)
    doc_index = jnp.sum((document_starts[None, :] <= positions[:, None]).astype(jnp.int32), axis=1) - 1
    doc_begin = jnp.any(document_starts[None, :] == positions[:, None], axis=1).astype(jnp.int32)
    decay_sum = jnp.cumsum(log_decay.reshape(LOCAL_HEADS, blocks, BLOCK), axis=-1)
    pair_weight, to_end, from_start, block_decay = block_factors(
        decay_sum, doc_index.reshape(blocks, BLOCK), doc_begin.reshape(blocks, BLOCK))
    keys_weighted = (keys_b * to_end[..., None]).astype(jnp.bfloat16).astype(jnp.float32)
    queries_weighted = (queries_b * from_start[..., None]).astype(jnp.bfloat16).astype(jnp.float32)
    key_state = jnp.einsum("hbse,hbsf->hbef", keys_weighted, values_b)
    query_state = jnp.einsum("hbte,hbtf->hbef", queries_weighted, upstream)

    def advance(state, item):
        decay_now, added = item
        return decay_now[:, None, None] * state + added, state

    empty = jnp.zeros((LOCAL_HEADS, HEAD_DIM, HEAD_DIM), jnp.float32)
    unused, before = lax.scan(advance, empty, (block_decay.T, key_state.swapaxes(0, 1)))
    unused, after = lax.scan(advance, empty, (block_decay.T, query_state.swapaxes(0, 1)), reverse=True)
    state_before = before.swapaxes(0, 1).astype(jnp.bfloat16).astype(jnp.float32)
    state_after = after.swapaxes(0, 1).astype(jnp.bfloat16).astype(jnp.float32)
    query_key = (jnp.einsum("hbte,hbse->hbts", queries_b, keys_b) * pair_weight).astype(jnp.bfloat16).astype(jnp.float32)
    value_score = (jnp.einsum("hbtf,hbsf->hbts", upstream, values_b) * pair_weight).astype(jnp.bfloat16).astype(jnp.float32)
    query_gradient = jnp.einsum("hbts,hbse->hbte", value_score, keys_b) + from_start[..., None] * jnp.einsum("hbtf,hbef->hbte", upstream, state_before)
    key_gradient = jnp.einsum("hbts,hbte->hbse", value_score, queries_b) + to_end[..., None] * jnp.einsum("hbsf,hbef->hbse", values_b, state_after)
    value_gradient = jnp.einsum("hbts,hbtf->hbsf", query_key, upstream) + to_end[..., None] * jnp.einsum("hbse,hbef->hbsf", keys_b, state_after)
    project_gradient = jnp.stack([
        merge_blocks(query_gradient) * silu_slope(projected[:, 0]) * query_scale,
        merge_blocks(key_gradient) * silu_slope(projected[:, 1]),
        merge_blocks(value_gradient)], axis=1).astype(jnp.bfloat16)
    group_cols = columns // N_HEAD
    grad_groups = project_gradient.reshape(PACKED_TOKENS, 3, N_HEAD, group_cols).transpose(2, 0, 1, 3)
    weight_groups = projection.reshape(D, 3, N_HEAD, group_cols).transpose(2, 0, 1, 3)

    def add_head_group(total, item):
        group_grad, group_weight = item
        head_partial = jnp.einsum("tkc,dkc->td", group_grad.astype(jnp.float32), group_weight.astype(jnp.float32))
        rounded = lax.optimization_barrier(head_partial.astype(jnp.bfloat16))
        return total + rounded.astype(jnp.float32), None

    summed, unused = lax.scan(add_head_group, jnp.zeros((PACKED_TOKENS, D), jnp.float32), (grad_groups, weight_groups))
    input_gradient = summed.astype(jnp.bfloat16)
    flat_gradient = project_gradient.reshape(PACKED_TOKENS, 3 * columns)
    grouped_inputs = inputs.reshape(N_SEQ, TOK_DEV, D)
    grouped_gradient = flat_gradient.reshape(N_SEQ, TOK_DEV, 3 * columns)

    def add_group(total, item):
        group_inputs, group_gradient = item
        partial_value = lax.dot_general(group_inputs, group_gradient, (((0,), (0,)), ((), ())),
                                  preferred_element_type=jnp.float32)
        rounded = lax.optimization_barrier(partial_value.astype(jnp.bfloat16))
        return total + rounded.astype(jnp.float32), None

    total, unused = lax.scan(add_group, jnp.zeros((D, 3 * columns), jnp.float32), (grouped_inputs, grouped_gradient))
    weight_gradient = total.astype(jnp.bfloat16).reshape(D, 3, columns)
    return input_gradient, weight_gradient
```

```python
import jax
import jax.numpy as jnp
from jax import lax
from jax.sharding import PartitionSpec as P

HEAD_DIM = 128
BLOCK = 256


def hop(array, axis, flip):
    return lax.ppermute(array, axis, [(i, i ^ flip) for i in range(lax.axis_size(axis))])


def gather_states(packed, axis):
    length = lax.axis_size(axis)
    if length != 4:
        return lax.all_gather(packed, axis)
    place = lax.axis_index(axis)
    parts = [packed] + [hop(packed, axis, flip) for flip in range(1, length)]
    rows = []
    for at in range(length):
        row = parts[0]
        for flip in range(1, length):
            row = jnp.where(place == (at ^ flip), parts[flip], row)
        rows.append(row)
    return rows


def combine_devices(states, decays, place, reverse):
    length = len(decays)
    total = jnp.zeros_like(states[0])
    for k in range(length):
        at = length - 1 - k if reverse else k
        reached = at > place if reverse else at < place
        total = jnp.where(reached, decays[at][:, None, None] * total + states[at], total)
    return total


def gather_rows(part, axis):
    length, place, rows = (lax.axis_size(axis), lax.axis_index(axis), part.shape[1])
    if length != 4:
        whole = lax.all_gather(part, axis, axis=1, tiled=True)
        return [(0, 0, whole)]
    half = rows // 2
    low, high = part[:, :half], part[:, half:]
    x_high = hop(high, axis, 1)
    y_low = hop(low, axis, 2)
    x_low = hop(low, axis, 1)
    y_high = hop(high, axis, 2)
    d_low = hop(y_low, axis, 1)
    d_high = hop(x_high, axis, 2)
    return [
        (place, 0, low),
        (place, half, high),
        (place ^ 1, half, x_high),
        (place ^ 2, 0, y_low),
        (place ^ 1, 0, x_low),
        (place ^ 2, half, y_high),
        (place ^ 3, 0, d_low),
        (place ^ 3, half, d_high),
    ]


def scatter_rows(partial, axis, rows):
    length, place = (lax.axis_size(axis), lax.axis_index(axis))
    if length != 4:
        return lax.psum_scatter(
            partial(0, 0, rows * length), axis, scatter_dimension=1, tiled=True
        )
    half = rows // 2

    def add(*terms):
        return sum(term.astype(jnp.float32) for term in terms).astype(jnp.bfloat16)

    far_low = hop(partial(place ^ 3, 0, half), axis, 1)
    far_high = hop(partial(place ^ 3, half, half), axis, 2)
    x_low = hop(partial(place ^ 1, 0, half), axis, 1)
    y_high = hop(partial(place ^ 2, half, half), axis, 2)
    x_high = hop(add(partial(place ^ 1, half, half), far_high), axis, 1)
    y_low = hop(add(partial(place ^ 2, 0, half), far_low), axis, 2)
    own_low, own_high = partial(place, 0, half), partial(place, half, half)
    return jnp.concatenate([add(own_low, x_low, y_low), add(own_high, x_high, y_high)], axis=1)


def silu_slope(point):
    sigma = jax.nn.sigmoid(point)
    return sigma * (1.0 + point * (1.0 - sigma))


def block_factors(decay_sum, doc_index, doc_begin):
    inside = jnp.arange(doc_index.shape[-1], dtype=jnp.int32)
    causal = inside[:, None] >= inside[None, :]
    same_doc = (doc_index[:, :, None] == doc_index[:, None, :]) & causal[None]
    spread = jnp.minimum(decay_sum[..., :, None] - decay_sum[..., None, :], 0.0)
    pair_weight = jnp.where(same_doc[None], jnp.exp(spread), 0.0)
    to_end = jnp.where(
        (doc_index == doc_index[:, -1:])[None], jnp.exp(decay_sum[..., -1:] - decay_sum), 0.0
    )
    began_flag = doc_index == doc_index[:, :1] - doc_begin[:, :1]
    from_start = jnp.where(began_flag[None], jnp.exp(decay_sum), 0.0)
    return (pair_weight, to_end, from_start, from_start[..., -1])


def block_pair(decay):
    high = decay.astype(jnp.bfloat16)
    low = (decay - high.astype(jnp.float32)).astype(jnp.bfloat16)
    pair = jnp.stack([high, low], axis=1)
    slab = jnp.pad(pair, ((0, HEAD_DIM - pair.shape[0]), (0, HEAD_DIM - 2)))
    return slab[None]


def combine_states(earlier, later):
    return (earlier[0] * later[0], later[0][:, None, None] * earlier[1] + later[1])


def body(inputs, projection, cotangent, log_decay, document_starts):
    tokens = inputs.shape[0]
    heads_here = log_decay.shape[0]
    local_cols = cotangent.shape[1]
    blocks = tokens // BLOCK
    query_scale = HEAD_DIM ** (-0.5)
    features = lax.all_gather(inputs, "head", axis=1, tiled=True)
    rows = projection.shape[0]
    blocks_w = gather_rows(projection.transpose(1, 0, 2), "seq")

    def feature_rows(owner, first, count):
        return lax.dynamic_slice_in_dim(features, owner * rows + first, count, axis=1)

    projected = sum(
        jnp.einsum(
            "td,kdc->ktc",
            feature_rows(owner, first, block.shape[1]),
            block,
            preferred_element_type=jnp.float32,
        )
        for owner, first, block in blocks_w
    )
    queries = (jax.nn.silu(projected[0]) * query_scale).astype(jnp.bfloat16)
    keys = jax.nn.silu(projected[1]).astype(jnp.bfloat16)
    values = projected[2].astype(jnp.bfloat16)

    def split_blocks(table):
        return table.reshape(blocks, BLOCK, heads_here, HEAD_DIM).transpose(2, 0, 1, 3)

    def merge_blocks(table):
        return table.transpose(1, 2, 0, 3).reshape(tokens, local_cols)

    queries_b = split_blocks(queries)
    keys_b = split_blocks(keys)
    values_b = split_blocks(values)
    upstream = split_blocks(cotangent)
    offset = lax.axis_index("seq") * tokens
    positions = offset + jnp.arange(tokens, dtype=jnp.int32)
    doc_index = (
        jnp.sum((document_starts[None, :] <= positions[:, None]).astype(jnp.int32), axis=1) - 1
    )
    doc_begin = jnp.any(document_starts[None, :] == positions[:, None], axis=1).astype(jnp.int32)
    decay_sum = jnp.cumsum(log_decay.reshape(heads_here, blocks, BLOCK), axis=-1)
    pair_weight, to_end, from_start, block_decay = block_factors(
        decay_sum, doc_index.reshape(blocks, BLOCK), doc_begin.reshape(blocks, BLOCK)
    )
    keys_weighted = (keys_b.astype(jnp.float32) * to_end[..., None]).astype(jnp.bfloat16)
    queries_weighted = (queries_b.astype(jnp.float32) * from_start[..., None]).astype(jnp.bfloat16)
    key_state = jnp.einsum(
        "hbse,hbsf->hbef", keys_weighted, values_b, preferred_element_type=jnp.float32
    )
    query_state = jnp.einsum(
        "hbte,hbtf->hbef", queries_weighted, upstream, preferred_element_type=jnp.float32
    )

    def local_step(carry, item):
        return (combine_states(carry, item), carry)

    ones = jnp.ones((heads_here,), jnp.float32)
    empty = jnp.zeros((heads_here, HEAD_DIM, HEAD_DIM), jnp.float32)
    (device_decay, device_keys), (prior_decay, prior_keys) = lax.scan(
        local_step, (ones, empty), (block_decay.T, key_state.swapaxes(0, 1))
    )
    (device_decay_back, device_query), (later_decay, later_query) = lax.scan(
        local_step, (ones, empty), (block_decay.T, query_state.swapaxes(0, 1)), reverse=True
    )
    place = lax.axis_index("seq")
    rough = block_pair(device_decay)
    packed = jnp.concatenate(
        [device_keys.astype(jnp.bfloat16), device_query.astype(jnp.bfloat16), rough]
    )
    everything = gather_states(packed, "seq")
    everything = [everything[k].astype(jnp.float32) for k in range(lax.axis_size("seq"))]
    decays = [
        part[2 * heads_here, :heads_here, 0] + part[2 * heads_here, :heads_here, 1]
        for part in everything
    ]
    forward_in = combine_devices([part[:heads_here] for part in everything], decays, place, False)
    backward_in = combine_devices(
        [part[heads_here : 2 * heads_here] for part in everything], decays, place, True
    )
    state_before = (
        (prior_decay[:, :, None, None] * forward_in[None] + prior_keys)
        .swapaxes(0, 1)
        .astype(jnp.bfloat16)
    )
    state_after = (
        (later_decay[:, :, None, None] * backward_in[None] + later_query)
        .swapaxes(0, 1)
        .astype(jnp.bfloat16)
    )
    query_key = (
        jnp.einsum("hbte,hbse->hbts", queries_b, keys_b, preferred_element_type=jnp.float32)
        * pair_weight
    ).astype(jnp.bfloat16)
    value_score = (
        jnp.einsum("hbtf,hbsf->hbts", upstream, values_b, preferred_element_type=jnp.float32)
        * pair_weight
    ).astype(jnp.bfloat16)
    query_gradient = jnp.einsum(
        "hbts,hbse->hbte", value_score, keys_b, preferred_element_type=jnp.float32
    ) + from_start[..., None] * jnp.einsum(
        "hbtf,hbef->hbte", upstream, state_before, preferred_element_type=jnp.float32
    )
    key_gradient = jnp.einsum(
        "hbts,hbte->hbse", value_score, queries_b, preferred_element_type=jnp.float32
    ) + to_end[..., None] * jnp.einsum(
        "hbsf,hbef->hbse", values_b, state_after, preferred_element_type=jnp.float32
    )
    value_gradient = jnp.einsum(
        "hbts,hbtf->hbsf", query_key, upstream, preferred_element_type=jnp.float32
    ) + to_end[..., None] * jnp.einsum(
        "hbse,hbef->hbsf", keys_b, state_after, preferred_element_type=jnp.float32
    )
    project_gradient = jnp.stack(
        [
            merge_blocks(query_gradient) * silu_slope(projected[0]) * query_scale,
            merge_blocks(key_gradient) * silu_slope(projected[1]),
            merge_blocks(value_gradient),
        ],
        axis=0,
    ).astype(jnp.bfloat16)
    def weight_partial(owner, first, count):
        return jnp.einsum(
            "td,ktc->kdc",
            feature_rows(owner, first, count),
            project_gradient,
            preferred_element_type=jnp.float32,
        ).astype(jnp.bfloat16)

    partial_value = jnp.zeros((tokens, features.shape[1]), jnp.bfloat16)
    for owner, first, block in blocks_w:
        piece = jnp.einsum(
            "ktc,kdc->td", project_gradient, block, preferred_element_type=jnp.float32
        ).astype(jnp.bfloat16)
        partial_value = lax.dynamic_update_slice_in_dim(
            partial_value, piece, owner * rows + first, axis=1
        )
    input_gradient = lax.psum_scatter(partial_value, "head", scatter_dimension=1, tiled=True)
    weight_gradient = scatter_rows(weight_partial, "seq", rows).transpose(1, 0, 2)
    return (input_gradient, weight_gradient)


def solution(mesh):
    placed = (P("seq", "head"), P("seq", None, "head"), P("seq", "head"), P("head", "seq"), P())
    return jax.shard_map(
        body,
        mesh=mesh,
        in_specs=placed,
        out_specs=(P("seq", "head"), P("seq", None, "head")),
        check_vma=False,
    )
```

```python
import jax
import jax.numpy as jnp
from jax import lax
from jax.experimental import pallas as pl
from jax.experimental.pallas import tpu as pltpu
from jax.sharding import PartitionSpec as P

HEAD_DIM = 128
BLOCK = 256


def hop(array, axis, flip):
    return lax.ppermute(array, axis, [(i, i ^ flip) for i in range(lax.axis_size(axis))])


def gather_states(packed, axis):
    length, place = (lax.axis_size(axis), lax.axis_index(axis))
    if length != 4:
        whole = lax.all_gather(packed, axis)
        return [whole[k] for k in range(length)], jnp.arange(length, dtype=jnp.int32)
    parts = [packed] + [hop(packed, axis, flip) for flip in range(1, length)]
    return parts, place ^ jnp.arange(length, dtype=jnp.int32)


def device_weights(device_decay, owners, axis):
    length, place = (lax.axis_size(axis), lax.axis_index(axis))
    decays = lax.all_gather(device_decay, axis)
    at, other = owners[:, None], jnp.arange(length, dtype=jnp.int32)[None]
    before = (other > at) & (other < place)
    after = (other < at) & (other > place)
    weights = []
    for between, counts in ((before, owners < place), (after, owners > place)):
        product = jnp.prod(jnp.where(between[:, :, None], decays[None], 1.0), axis=1)
        weights.append(jnp.where(counts[:, None], product, 0.0))
    return jnp.stack(weights)


def gather_rows(part, axis):
    length, place, rows = (lax.axis_size(axis), lax.axis_index(axis), part.shape[1])
    if length != 4:
        whole = lax.all_gather(part, axis, axis=1, tiled=True)
        return [(0, 0, whole)]
    half = rows // 2
    low, high = part[:, :half], part[:, half:]
    x_high = hop(high, axis, 1)
    y_low = hop(low, axis, 2)
    x_low = hop(low, axis, 1)
    y_high = hop(high, axis, 2)
    d_low = hop(y_low, axis, 1)
    d_high = hop(x_high, axis, 2)
    return [
        (place, 0, low),
        (place, half, high),
        (place ^ 1, half, x_high),
        (place ^ 2, 0, y_low),
        (place ^ 1, 0, x_low),
        (place ^ 2, half, y_high),
        (place ^ 3, 0, d_low),
        (place ^ 3, half, d_high),
    ]


def scatter_rows(partial, between, source, axis, rows):
    length, place = (lax.axis_size(axis), lax.axis_index(axis))
    if length != 4:
        whole = partial(source, 0, 0, rows * length)
        return between(source), lax.psum_scatter(whole, axis, scatter_dimension=1, tiled=True)
    half = rows // 2

    def add(*terms):
        return sum(term.astype(jnp.float32) for term in terms).astype(jnp.bfloat16)

    far_low, far_high = partial(source, place ^ 3, 0, half), partial(source, place ^ 3, half, half)
    source, far_low, far_high = lax.optimization_barrier((source, far_low, far_high))
    far_low, far_high = hop(far_low, axis, 1), hop(far_high, axis, 2)
    beside = between(source)
    source, beside = lax.optimization_barrier((source, beside))
    x_low = hop(partial(source, place ^ 1, 0, half), axis, 1)
    y_high = hop(partial(source, place ^ 2, half, half), axis, 2)
    x_high = hop(add(partial(source, place ^ 1, half, half), far_high), axis, 1)
    y_low = hop(add(partial(source, place ^ 2, 0, half), far_low), axis, 2)
    own_low, own_high = partial(source, place, 0, half), partial(source, place, half, half)
    whole = jnp.concatenate([add(own_low, x_low, y_low), add(own_high, x_high, y_high)], axis=1)
    return beside, whole


def block_factors(decay_sum, doc_index, doc_begin):
    inside = jnp.arange(doc_index.shape[-1], dtype=jnp.int32)
    causal = inside[:, None] >= inside[None, :]
    same_doc = (doc_index[:, :, None] == doc_index[:, None, :]) & causal[None]
    spread = jnp.minimum(decay_sum[..., :, None] - decay_sum[..., None, :], 0.0)
    pair_weight = jnp.where(same_doc[None], jnp.exp(spread), 0.0)
    to_end = jnp.where(
        (doc_index == doc_index[:, -1:])[None], jnp.exp(decay_sum[..., -1:] - decay_sum), 0.0
    )
    began_flag = doc_index == doc_index[:, :1] - doc_begin[:, :1]
    from_start = jnp.where(began_flag[None], jnp.exp(decay_sum), 0.0)
    return (pair_weight, to_end, from_start, from_start[..., -1])


def dot(left, right, contract):
    return lax.dot_general(
        left, right, ((contract[:1], contract[1:]), ((), ())), preferred_element_type=jnp.float32
    )


def projections(proj_ref, span):
    point_q, point_k = proj_ref[0, span], proj_ref[1, span]
    gate_q, gate_k = jax.nn.sigmoid(point_q), jax.nn.sigmoid(point_k)
    queries = (point_q * gate_q * HEAD_DIM ** (-0.5)).astype(jnp.bfloat16)
    keys = (point_k * gate_k).astype(jnp.bfloat16)
    values = proj_ref[2, span].astype(jnp.bfloat16)
    return (point_q, gate_q, queries), (point_k, gate_k, keys), values


def state_kernel(proj_ref, up_ref, start_ref, end_ref, key_ref, query_ref, total_ref):
    blocks = key_ref.shape[1]
    forward = jnp.zeros((HEAD_DIM, HEAD_DIM), jnp.float32)
    query_states, decays = [], []
    for b in range(blocks):
        span = pl.ds(b * BLOCK, BLOCK)
        (_, _, queries), (_, _, keys), values = projections(proj_ref, span)
        keys_weighted = (keys.astype(jnp.float32) * end_ref[0, span]).astype(jnp.bfloat16)
        queries_weighted = (queries.astype(jnp.float32) * start_ref[0, span]).astype(jnp.bfloat16)
        key_state = dot(keys_weighted, values, (0, 0))
        query_state = dot(queries_weighted, up_ref[span], (0, 0))
        key_ref[0, b] = key_state
        query_ref[0, b] = query_state
        decay = start_ref[0, pl.ds(b * BLOCK + BLOCK - 1, 1)]
        forward = decay * forward + key_state
        query_states.append(query_state)
        decays.append(decay)
    backward = jnp.zeros((HEAD_DIM, HEAD_DIM), jnp.float32)
    for b in reversed(range(blocks)):
        backward = decays[b] * backward + query_states[b]
    total_ref[0, 0] = forward.astype(jnp.bfloat16)
    total_ref[1, 0] = backward.astype(jnp.bfloat16)


def gradient_kernel(
    weight_ref, proj_ref, up_ref, start_ref, end_ref, pair_ref, key_ref, query_ref, *rest
):
    totals, out_ref = rest[:-1], rest[-1]
    blocks = key_ref.shape[1]
    head = pl.program_id(0)
    state = jnp.zeros((HEAD_DIM, HEAD_DIM), jnp.float32)
    reverse = jnp.zeros((HEAD_DIM, HEAD_DIM), jnp.float32)
    for k, total in enumerate(totals):
        state = state + weight_ref[0, k, head] * total[0, 0].astype(jnp.float32)
        reverse = reverse + weight_ref[1, k, head] * total[1, 0].astype(jnp.float32)
    decays = [start_ref[0, pl.ds(b * BLOCK + BLOCK - 1, 1)] for b in range(blocks)]
    after = [None] * blocks
    for b in reversed(range(blocks)):
        after[b] = reverse.astype(jnp.bfloat16)
        reverse = decays[b] * reverse + query_ref[0, b]
    for b in range(blocks):
        before = state.astype(jnp.bfloat16)
        state = decays[b] * state + key_ref[0, b]
        span = pl.ds(b * BLOCK, BLOCK)
        (point_q, gate_q, queries), (point_k, gate_k, keys), values = projections(proj_ref, span)
        upstream = up_ref[span]
        from_start, to_end, pair = start_ref[0, span], end_ref[0, span], pair_ref[0, b]
        query_key = (dot(queries, keys, (1, 1)) * pair).astype(jnp.bfloat16)
        value_score = (dot(upstream, values, (1, 1)) * pair).astype(jnp.bfloat16)
        query_gradient = dot(value_score, keys, (1, 0)) + from_start * dot(
            upstream, before, (1, 1)
        )
        key_gradient = dot(value_score, queries, (0, 0)) + to_end * dot(values, after[b], (1, 1))
        value_gradient = dot(query_key, upstream, (0, 0)) + to_end * dot(keys, after[b], (1, 0))
        slope_q = gate_q * (1.0 + point_q * (1.0 - gate_q)) * HEAD_DIM ** (-0.5)
        slope_k = gate_k * (1.0 + point_k * (1.0 - gate_k))
        out_ref[0, span] = (query_gradient * slope_q).astype(jnp.bfloat16)
        out_ref[1, span] = (key_gradient * slope_k).astype(jnp.bfloat16)
        out_ref[2, span] = value_gradient.astype(jnp.bfloat16)


def input_kernel(gradient_ref, weight_ref, out_ref):
    for first in range(0, out_ref.shape[0], BLOCK):
        span = pl.ds(first, BLOCK)
        total = dot(gradient_ref[0, span], weight_ref[0], (1, 1))
        for k in (1, 2):
            total = total + dot(gradient_ref[k, span], weight_ref[k], (1, 1))
        out_ref[span] = total.astype(jnp.bfloat16)


def body(inputs, projection, cotangent, log_decay, document_starts):
    tokens = inputs.shape[0]
    heads_here = log_decay.shape[0]
    local_cols = cotangent.shape[1]
    blocks = tokens // BLOCK
    features = lax.all_gather(inputs, "head", axis=1, tiled=True)
    rows = projection.shape[0]
    blocks_w = gather_rows(projection.transpose(1, 0, 2), "seq")

    def feature_rows(owner, first, count):
        return lax.dynamic_slice_in_dim(features, owner * rows + first, count, axis=1)

    projected = None
    weights_all = jnp.zeros((3, features.shape[1], local_cols), jnp.bfloat16)
    for owner, first, block in blocks_w:
        piece = jnp.einsum(
            "td,kdc->ktc",
            feature_rows(owner, first, block.shape[1]),
            block,
            preferred_element_type=jnp.float32,
        )
        projected = piece if projected is None else lax.optimization_barrier(projected) + piece
        weights_all = lax.dynamic_update_slice_in_dim(
            weights_all, block, owner * rows + first, axis=1
        )
    offset = lax.axis_index("seq") * tokens
    positions = offset + jnp.arange(tokens, dtype=jnp.int32)
    doc_index = (
        jnp.sum((document_starts[None, :] <= positions[:, None]).astype(jnp.int32), axis=1) - 1
    )
    doc_begin = jnp.any(document_starts[None, :] == positions[:, None], axis=1).astype(jnp.int32)
    decay_sum = jnp.cumsum(log_decay.reshape(heads_here, blocks, BLOCK), axis=-1)
    pair_weight, to_end, from_start, block_decay = block_factors(
        decay_sum, doc_index.reshape(blocks, BLOCK), doc_begin.reshape(blocks, BLOCK)
    )
    lanes = (heads_here, tokens, HEAD_DIM)
    to_end = jnp.broadcast_to(to_end.reshape(heads_here, tokens)[..., None], lanes)
    from_start = jnp.broadcast_to(from_start.reshape(heads_here, tokens)[..., None], lanes)
    device_decay = jnp.prod(block_decay, axis=1)

    proj_spec = pl.BlockSpec((3, tokens, HEAD_DIM), lambda h: (0, 0, h))
    up_spec = pl.BlockSpec((tokens, HEAD_DIM), lambda h: (0, h))
    lane_spec = pl.BlockSpec((1, tokens, HEAD_DIM), lambda h: (h, 0, 0))
    state_spec = pl.BlockSpec((1, blocks, HEAD_DIM, HEAD_DIM), lambda h: (h, 0, 0, 0))
    total_spec = pl.BlockSpec((2, 1, HEAD_DIM, HEAD_DIM), lambda h: (0, h, 0, 0))
    pair_spec = pl.BlockSpec((1, blocks, BLOCK, BLOCK), lambda h: (h, 0, 0, 0))
    states = jax.ShapeDtypeStruct((heads_here, blocks, HEAD_DIM, HEAD_DIM), jnp.float32)
    key_state, query_state, totals = pl.pallas_call(
        state_kernel,
        grid=(heads_here,),
        in_specs=[proj_spec, up_spec, lane_spec, lane_spec],
        out_specs=[state_spec, state_spec, total_spec],
        out_shape=[
            states,
            states,
            jax.ShapeDtypeStruct((2, heads_here, HEAD_DIM, HEAD_DIM), jnp.bfloat16),
        ],
    )(projected, cotangent, from_start, to_end)
    parts, owners = gather_states(totals, "seq")
    weights = device_weights(device_decay, owners, "seq")
    project_gradient = pl.pallas_call(
        gradient_kernel,
        grid=(heads_here,),
        in_specs=[pl.BlockSpec(memory_space=pltpu.SMEM)]
        + [proj_spec, up_spec, lane_spec, lane_spec, pair_spec, state_spec, state_spec]
        + [total_spec] * len(parts),
        out_specs=proj_spec,
        out_shape=jax.ShapeDtypeStruct(projected.shape, jnp.bfloat16),
    )(weights, projected, cotangent, from_start, to_end, pair_weight, key_state, query_state, *parts)

    def weight_partial(gradient, owner, first, count):
        return jnp.einsum(
            "td,ktc->kdc",
            feature_rows(owner, first, count),
            gradient,
            preferred_element_type=jnp.float32,
        ).astype(jnp.bfloat16)

    def input_partial(gradient):
        columns = features.shape[1]
        tile = columns // 8
        return pl.pallas_call(
            input_kernel,
            grid=(columns // tile,),
            in_specs=[
                pl.BlockSpec(gradient.shape, lambda i: (0, 0, 0)),
                pl.BlockSpec((3, tile, local_cols), lambda i: (0, i, 0)),
            ],
            out_specs=pl.BlockSpec((tokens, tile), lambda i: (0, i)),
            out_shape=jax.ShapeDtypeStruct((tokens, columns), jnp.bfloat16),
            cost_estimate=pl.CostEstimate(flops=1, bytes_accessed=1, transcendentals=0),
            compiler_params=pltpu.CompilerParams(vmem_limit_bytes=40 << 20),
        )(gradient, weights_all)

    partial_value, weight_gradient = scatter_rows(
        weight_partial, input_partial, project_gradient, "seq", rows
    )
    input_gradient = lax.psum_scatter(partial_value, "head", scatter_dimension=1, tiled=True)
    weight_gradient = weight_gradient.transpose(1, 0, 2)
    return (input_gradient, weight_gradient)


def solution(mesh):
    placed = (P("seq", "head"), P("seq", None, "head"), P("seq", "head"), P("head", "seq"), P())
    return jax.shard_map(
        body,
        mesh=mesh,
        in_specs=placed,
        out_specs=(P("seq", "head"), P("seq", None, "head")),
        check_vma=False,
    )
```

```python
import jax
import jax.numpy as jnp
from jax import lax
from jax.experimental import pallas as pl
from jax.experimental.layout import Layout, with_layout_constraint
from jax.experimental.pallas import tpu as pltpu
from jax.sharding import PartitionSpec as P

HEAD_DIM = 128
BLOCK = 256


def hop(array, axis, flip):
    return lax.ppermute(array, axis, [(i, i ^ flip) for i in range(lax.axis_size(axis))])


def gather_states(packed, axis):
    length, place = (lax.axis_size(axis), lax.axis_index(axis))
    if length != 4:
        whole = lax.all_gather(packed, axis)
        return [whole[k] for k in range(length)], jnp.arange(length, dtype=jnp.int32)
    parts = [packed] + [hop(packed, axis, flip) for flip in range(1, length)]
    return parts, place ^ jnp.arange(length, dtype=jnp.int32)


def device_weights(device_decay, owners, axis):
    length, place = (lax.axis_size(axis), lax.axis_index(axis))
    if length == 4:
        slab = jnp.broadcast_to(device_decay[:, None], (device_decay.shape[0], HEAD_DIM))
        hops = [slab] + [hop(slab, axis, flip) for flip in range(1, length)]
        arrived = jnp.stack([part[:, 0] for part in hops])
        mine = owners[None, :] == jnp.arange(length, dtype=jnp.int32)[:, None]
        decays = jnp.sum(jnp.where(mine[:, :, None], arrived[None], 0.0), axis=1)
    else:
        decays = lax.all_gather(device_decay, axis)
    at, other = owners[:, None], jnp.arange(length, dtype=jnp.int32)[None]
    before = (other > at) & (other < place)
    after = (other < at) & (other > place)
    weights = []
    for between, counts in ((before, owners < place), (after, owners > place)):
        product = jnp.prod(jnp.where(between[:, :, None], decays[None], 1.0), axis=1)
        weights.append(jnp.where(counts[:, None], product, 0.0))
    return jnp.stack(weights)


def gather_rows(part, axis):
    length, place, rows = (lax.axis_size(axis), lax.axis_index(axis), part.shape[1])
    if length != 4:
        whole = lax.all_gather(part, axis, axis=1, tiled=True)
        return [(0, 0, whole)]
    half = rows // 2
    low, high = part[:, :half], part[:, half:]
    x_high = hop(high, axis, 1)
    y_low = hop(low, axis, 2)
    x_low = hop(low, axis, 1)
    y_high = hop(high, axis, 2)
    d_low = hop(y_low, axis, 1)
    d_high = hop(x_high, axis, 2)
    return [
        (place, 0, low),
        (place, half, high),
        (place ^ 1, half, x_high),
        (place ^ 2, 0, y_low),
        (place ^ 1, 0, x_low),
        (place ^ 2, half, y_high),
        (place ^ 3, 0, d_low),
        (place ^ 3, half, d_high),
    ]


def scatter_rows(partial, between, source, axis, rows):
    length, place = (lax.axis_size(axis), lax.axis_index(axis))
    if length != 4:
        whole = partial(source, 0, 0, rows * length)
        return [between(source, 0, 1)], lax.psum_scatter(whole, axis, scatter_dimension=1, tiled=True)
    half = rows // 2

    def add(*terms):
        return sum(term.astype(jnp.float32) for term in terms).astype(jnp.bfloat16)

    far_low, far_high = partial(source, place ^ 3, 0, half), partial(source, place ^ 3, half, half)
    source, far_low, far_high = lax.optimization_barrier((source, far_low, far_high))
    far_low, far_high = hop(far_low, axis, 1), hop(far_high, axis, 2)
    beside = between(source, 0, 1)
    source, beside = lax.optimization_barrier((source, beside))
    x_low, y_high = partial(source, place ^ 1, 0, half), partial(source, place ^ 2, half, half)
    source, x_low, y_high = lax.optimization_barrier((source, x_low, y_high))
    x_low, y_high = hop(x_low, axis, 1), hop(y_high, axis, 2)
    x_high = hop(add(partial(source, place ^ 1, half, half), far_high), axis, 1)
    y_low = hop(add(partial(source, place ^ 2, 0, half), far_low), axis, 2)
    own_low, own_high = partial(source, place, 0, half), partial(source, place, half, half)
    whole = jnp.concatenate([add(own_low, x_low, y_low), add(own_high, x_high, y_high)], axis=1)
    return [beside], whole


def block_factors(decay_sum, doc_index, doc_begin):
    inside = jnp.arange(doc_index.shape[-1], dtype=jnp.int32)
    causal = inside[:, None] >= inside[None, :]
    same_doc = (doc_index[:, :, None] == doc_index[:, None, :]) & causal[None]
    spread = jnp.minimum(decay_sum[..., :, None] - decay_sum[..., None, :], 0.0)
    pair_weight = jnp.where(same_doc[None], jnp.exp(spread), 0.0)
    to_end = jnp.where(
        (doc_index == doc_index[:, -1:])[None], jnp.exp(decay_sum[..., -1:] - decay_sum), 0.0
    )
    began_flag = doc_index == doc_index[:, :1] - doc_begin[:, :1]
    from_start = jnp.where(began_flag[None], jnp.exp(decay_sum), 0.0)
    return (pair_weight, to_end, from_start, from_start[..., -1])


def dot(left, right, contract):
    return lax.dot_general(
        left, right, ((contract[:1], contract[1:]), ((), ())), preferred_element_type=jnp.float32
    )


def projections(proj_ref, span):
    point_q, point_k = proj_ref[0, span], proj_ref[1, span]
    gate_q, gate_k = jax.nn.sigmoid(point_q), jax.nn.sigmoid(point_k)
    queries = (point_q * gate_q * HEAD_DIM ** (-0.5)).astype(jnp.bfloat16)
    keys = (point_k * gate_k).astype(jnp.bfloat16)
    values = proj_ref[2, span].astype(jnp.bfloat16)
    return (point_q, gate_q, queries), (point_k, gate_k, keys), values


def state_kernel(proj_ref, up_ref, start_ref, end_ref, key_ref, query_ref, total_ref):
    blocks = key_ref.shape[1]
    forward = jnp.zeros((HEAD_DIM, HEAD_DIM), jnp.float32)
    query_states, decays = [], []
    for b in range(blocks):
        span = pl.ds(b * BLOCK, BLOCK)
        (_, _, queries), (_, _, keys), values = projections(proj_ref, span)
        keys_weighted = (keys.astype(jnp.float32) * end_ref[0, span]).astype(jnp.bfloat16)
        queries_weighted = (queries.astype(jnp.float32) * start_ref[0, span]).astype(jnp.bfloat16)
        key_state = dot(keys_weighted, values, (0, 0))
        query_state = dot(queries_weighted, up_ref[span], (0, 0))
        key_ref[0, b] = key_state
        query_ref[0, b] = query_state
        decay = start_ref[0, pl.ds(b * BLOCK + BLOCK - 1, 1)]
        forward = decay * forward + key_state
        query_states.append(query_state)
        decays.append(decay)
    backward = jnp.zeros((HEAD_DIM, HEAD_DIM), jnp.float32)
    for b in reversed(range(blocks)):
        backward = decays[b] * backward + query_states[b]
    total_ref[0, 0] = forward.astype(jnp.bfloat16)
    total_ref[1, 0] = backward.astype(jnp.bfloat16)


def gradient_kernel(
    weight_ref, proj_ref, up_ref, start_ref, end_ref, pair_ref, key_ref, query_ref, *rest
):
    totals, out_ref = rest[:-1], rest[-1]
    blocks = key_ref.shape[1]
    head = pl.program_id(0)
    state = jnp.zeros((HEAD_DIM, HEAD_DIM), jnp.float32)
    reverse = jnp.zeros((HEAD_DIM, HEAD_DIM), jnp.float32)
    for k, total in enumerate(totals):
        state = state + weight_ref[0, k, head] * total[0, 0].astype(jnp.float32)
        reverse = reverse + weight_ref[1, k, head] * total[1, 0].astype(jnp.float32)
    decays = [start_ref[0, pl.ds(b * BLOCK + BLOCK - 1, 1)] for b in range(blocks)]
    after = [None] * blocks
    for b in reversed(range(blocks)):
        after[b] = reverse.astype(jnp.bfloat16)
        reverse = decays[b] * reverse + query_ref[0, b]
    for b in range(blocks):
        before = state.astype(jnp.bfloat16)
        state = decays[b] * state + key_ref[0, b]
        span = pl.ds(b * BLOCK, BLOCK)
        (point_q, gate_q, queries), (point_k, gate_k, keys), values = projections(proj_ref, span)
        upstream = up_ref[span]
        from_start, to_end, pair = start_ref[0, span], end_ref[0, span], pair_ref[0, b]
        query_key = (dot(queries, keys, (1, 1)) * pair).astype(jnp.bfloat16)
        value_score = (dot(upstream, values, (1, 1)) * pair).astype(jnp.bfloat16)
        query_gradient = dot(value_score, keys, (1, 0)) + from_start * dot(
            upstream, before, (1, 1)
        )
        key_gradient = dot(value_score, queries, (0, 0)) + to_end * dot(values, after[b], (1, 1))
        value_gradient = dot(query_key, upstream, (0, 0)) + to_end * dot(keys, after[b], (1, 0))
        slope_q = gate_q * (1.0 + point_q * (1.0 - gate_q)) * HEAD_DIM ** (-0.5)
        slope_k = gate_k * (1.0 + point_k * (1.0 - gate_k))
        out_ref[0, span] = (query_gradient * slope_q).astype(jnp.bfloat16)
        out_ref[1, span] = (key_gradient * slope_k).astype(jnp.bfloat16)
        out_ref[2, span] = value_gradient.astype(jnp.bfloat16)


def input_kernel(gradient_ref, weight_ref, out_ref):
    for first in range(0, out_ref.shape[0], BLOCK):
        span = pl.ds(first, BLOCK)
        total = dot(gradient_ref[0, span], weight_ref[0], (1, 1))
        for k in (1, 2):
            total = total + dot(gradient_ref[k, span], weight_ref[k], (1, 1))
        out_ref[span] = total.astype(jnp.bfloat16)


def body(inputs, projection, cotangent, log_decay, document_starts):
    tokens = inputs.shape[0]
    heads_here = log_decay.shape[0]
    local_cols = cotangent.shape[1]
    blocks = tokens // BLOCK
    features = lax.all_gather(inputs, "head", axis=1, tiled=True)
    rows = projection.shape[0]
    blocks_w = gather_rows(projection.transpose(1, 0, 2), "seq")

    def feature_rows(owner, first, count):
        return lax.dynamic_slice_in_dim(features, owner * rows + first, count, axis=1)

    offset = lax.axis_index("seq") * tokens
    positions = offset + jnp.arange(tokens, dtype=jnp.int32)
    doc_index = (
        jnp.sum((document_starts[None, :] <= positions[:, None]).astype(jnp.int32), axis=1) - 1
    )
    doc_begin = jnp.any(document_starts[None, :] == positions[:, None], axis=1).astype(jnp.int32)
    decay_sum = jnp.cumsum(log_decay.reshape(heads_here, blocks, BLOCK), axis=-1)
    pair_weight, to_end, from_start, block_decay = block_factors(
        decay_sum, doc_index.reshape(blocks, BLOCK), doc_begin.reshape(blocks, BLOCK)
    )
    lanes = (heads_here, tokens, HEAD_DIM)
    to_end = jnp.broadcast_to(to_end.reshape(heads_here, tokens)[..., None], lanes)
    from_start = jnp.broadcast_to(from_start.reshape(heads_here, tokens)[..., None], lanes)
    device_decay = jnp.prod(block_decay, axis=1)

    zero = jnp.zeros((), jnp.bfloat16)
    if len(blocks_w) > 2:
        owner, first, block = blocks_w[2]
        zero, block = lax.optimization_barrier((zero, block))
        blocks_w[2] = (owner, first, block)
    weights_all = jnp.broadcast_to(zero, (3, features.shape[1], local_cols))

    def place_rows(whole, some):
        for owner, first, block in some:
            whole = lax.dynamic_update_slice_in_dim(whole, block, owner * rows + first, axis=1)
        return whole

    early, late = blocks_w[:6], blocks_w[6:]
    weights_all = place_rows(weights_all, early)
    features, weights_all, from_start, to_end, pair_weight = lax.optimization_barrier(
        (features, weights_all, from_start, to_end, pair_weight)
    )
    projected = None
    for k, (owner, first, block) in enumerate(blocks_w):
        piece = jnp.einsum(
            "td,kdc->ktc",
            feature_rows(owner, first, block.shape[1]),
            block,
            preferred_element_type=jnp.float32,
        )
        projected = piece if projected is None else lax.optimization_barrier(projected) + piece
        if k == min(5, len(blocks_w) - 1):
            projected, device_decay = lax.optimization_barrier((projected, device_decay))
    weights_all = place_rows(weights_all, late)

    proj_spec = pl.BlockSpec((3, tokens, HEAD_DIM), lambda h: (0, 0, h))
    up_spec = pl.BlockSpec((tokens, HEAD_DIM), lambda h: (0, h))
    lane_spec = pl.BlockSpec((1, tokens, HEAD_DIM), lambda h: (h, 0, 0))
    state_spec = pl.BlockSpec((1, blocks, HEAD_DIM, HEAD_DIM), lambda h: (h, 0, 0, 0))
    total_spec = pl.BlockSpec((2, 1, HEAD_DIM, HEAD_DIM), lambda h: (0, h, 0, 0))
    pair_spec = pl.BlockSpec((1, blocks, BLOCK, BLOCK), lambda h: (h, 0, 0, 0))
    states = jax.ShapeDtypeStruct((heads_here, blocks, HEAD_DIM, HEAD_DIM), jnp.float32)
    key_state, query_state, totals = pl.pallas_call(
        state_kernel,
        grid=(heads_here,),
        in_specs=[proj_spec, up_spec, lane_spec, lane_spec],
        out_specs=[state_spec, state_spec, total_spec],
        out_shape=[
            states,
            states,
            jax.ShapeDtypeStruct((2, heads_here, HEAD_DIM, HEAD_DIM), jnp.bfloat16),
        ],
    )(projected, cotangent, from_start, to_end)
    parts, owners = gather_states(totals, "seq")
    weights = device_weights(device_decay, owners, "seq")
    project_gradient = pl.pallas_call(
        gradient_kernel,
        grid=(heads_here,),
        in_specs=[pl.BlockSpec(memory_space=pltpu.SMEM)]
        + [proj_spec, up_spec, lane_spec, lane_spec, pair_spec, state_spec, state_spec]
        + [total_spec] * len(parts),
        out_specs=proj_spec,
        out_shape=jax.ShapeDtypeStruct(projected.shape, jnp.bfloat16),
    )(weights, projected, cotangent, from_start, to_end, pair_weight, key_state, query_state, *parts)

    def weight_partial(gradient, owner, first, count):
        term = jnp.einsum(
            "td,ktc->kdc",
            feature_rows(owner, first, count),
            gradient,
            preferred_element_type=jnp.float32,
        ).astype(jnp.bfloat16)
        return with_layout_constraint(term, Layout(major_to_minor=(0, 1, 2)))

    def input_partial(gradient, part, of):
        columns = features.shape[1]
        tile, count = columns // 8, tokens // of
        return pl.pallas_call(
            input_kernel,
            grid=(columns // tile,),
            in_specs=[
                pl.BlockSpec((3, count, local_cols), lambda i: (0, part, 0)),
                pl.BlockSpec((3, tile, local_cols), lambda i: (0, i, 0)),
            ],
            out_specs=pl.BlockSpec((count, tile), lambda i: (0, i)),
            out_shape=jax.ShapeDtypeStruct((count, columns), jnp.bfloat16),
            cost_estimate=pl.CostEstimate(flops=1, bytes_accessed=1, transcendentals=0),
            compiler_params=pltpu.CompilerParams(vmem_limit_bytes=40 << 20),
        )(gradient, weights_all)

    input_partials, weight_gradient = scatter_rows(
        weight_partial, input_partial, project_gradient, "seq", rows
    )
    input_gradient = lax.psum_scatter(
        input_partials[0], "head", scatter_dimension=1, tiled=True
    )
    weight_gradient = weight_gradient.transpose(1, 0, 2)
    return (input_gradient, weight_gradient)


def solution(mesh):
    placed = (P("seq", "head"), P("seq", None, "head"), P("seq", "head"), P("head", "seq"), P())
    return jax.shard_map(
        body,
        mesh=mesh,
        in_specs=placed,
        out_specs=(P("seq", "head"), P("seq", None, "head")),
        check_vma=False,
    )
```

```python
import jax
import jax.numpy as jnp
from jax import lax
from jax.experimental import pallas as pl
from jax.experimental.layout import Layout, with_layout_constraint
from jax.experimental.pallas import tpu as pltpu
from jax.sharding import PartitionSpec as P

HEAD_DIM = 128
BLOCK = 256


def hop(array, axis, flip):
    return lax.ppermute(array, axis, [(i, i ^ flip) for i in range(lax.axis_size(axis))])


def gather_states(packed, axis):
    length, place = (lax.axis_size(axis), lax.axis_index(axis))
    if length != 4:
        whole = lax.all_gather(packed, axis)
        return [whole[k] for k in range(length)], jnp.arange(length, dtype=jnp.int32)
    parts = [packed] + [hop(packed, axis, flip) for flip in range(1, length)]
    return parts, place ^ jnp.arange(length, dtype=jnp.int32)


def device_weights(device_decay, owners, axis):
    length, place = (lax.axis_size(axis), lax.axis_index(axis))
    if length == 4:
        slab = jnp.broadcast_to(device_decay[:, None], (device_decay.shape[0], HEAD_DIM))
        hops = [slab] + [hop(slab, axis, flip) for flip in range(1, length)]
        arrived = jnp.stack([part[:, 0] for part in hops])
        mine = owners[None, :] == jnp.arange(length, dtype=jnp.int32)[:, None]
        decays = jnp.sum(jnp.where(mine[:, :, None], arrived[None], 0.0), axis=1)
    else:
        decays = lax.all_gather(device_decay, axis)
    at, other = owners[:, None], jnp.arange(length, dtype=jnp.int32)[None]
    before = (other > at) & (other < place)
    after = (other < at) & (other > place)
    weights = []
    for between, counts in ((before, owners < place), (after, owners > place)):
        product = jnp.prod(jnp.where(between[:, :, None], decays[None], 1.0), axis=1)
        weights.append(jnp.where(counts[:, None], product, 0.0))
    return jnp.stack(weights)


def gather_rows(part, axis):
    length, place, rows = (lax.axis_size(axis), lax.axis_index(axis), part.shape[1])
    if length != 4:
        whole = lax.all_gather(part, axis, axis=1, tiled=True)
        return [(0, 0, whole)]
    half = rows // 2
    low, high = part[:, :half], part[:, half:]
    x_high = hop(high, axis, 1)
    y_low = hop(low, axis, 2)
    x_low = hop(low, axis, 1)
    y_high = hop(high, axis, 2)
    d_low = hop(y_low, axis, 1)
    d_high = hop(x_high, axis, 2)
    return [
        (place, 0, low),
        (place, half, high),
        (place ^ 1, half, x_high),
        (place ^ 2, 0, y_low),
        (place ^ 1, 0, x_low),
        (place ^ 2, half, y_high),
        (place ^ 3, 0, d_low),
        (place ^ 3, half, d_high),
    ]


def scatter_rows(partial, between, source, axis, rows):
    length, place = (lax.axis_size(axis), lax.axis_index(axis))
    if length != 4:
        whole = partial(source, 0, 0, rows * length)
        return [between(source, 0, 1)], lax.psum_scatter(whole, axis, scatter_dimension=1, tiled=True)
    half = rows // 2

    def add(*terms):
        return sum(term.astype(jnp.float32) for term in terms).astype(jnp.bfloat16)

    far_low, far_high = partial(source, place ^ 3, 0, half), partial(source, place ^ 3, half, half)
    source, far_low, far_high = lax.optimization_barrier((source, far_low, far_high))
    far_low, far_high = hop(far_low, axis, 1), hop(far_high, axis, 2)
    beside = between(source, 0, 1)
    source, beside = lax.optimization_barrier((source, beside))
    x_low, y_high = partial(source, place ^ 1, 0, half), partial(source, place ^ 2, half, half)
    source, x_low, y_high = lax.optimization_barrier((source, x_low, y_high))
    x_low, y_high = hop(x_low, axis, 1), hop(y_high, axis, 2)
    x_high = hop(add(partial(source, place ^ 1, half, half), far_high), axis, 1)
    y_low = hop(add(partial(source, place ^ 2, 0, half), far_low), axis, 2)
    own_low, own_high = partial(source, place, 0, half), partial(source, place, half, half)
    whole = jnp.concatenate([add(own_low, x_low, y_low), add(own_high, x_high, y_high)], axis=1)
    return [beside], whole


def block_factors(decay_sum, doc_index, doc_begin):
    inside = jnp.arange(doc_index.shape[-1], dtype=jnp.int32)
    causal = inside[:, None] >= inside[None, :]
    same_doc = (doc_index[:, :, None] == doc_index[:, None, :]) & causal[None]
    spread = jnp.minimum(decay_sum[..., :, None] - decay_sum[..., None, :], 0.0)
    pair_weight = jnp.where(same_doc[None], jnp.exp(spread), 0.0)
    to_end = jnp.where(
        (doc_index == doc_index[:, -1:])[None], jnp.exp(decay_sum[..., -1:] - decay_sum), 0.0
    )
    began_flag = doc_index == doc_index[:, :1] - doc_begin[:, :1]
    from_start = jnp.where(began_flag[None], jnp.exp(decay_sum), 0.0)
    return (pair_weight, to_end, from_start, from_start[..., -1])


def dot(left, right, contract):
    return lax.dot_general(
        left, right, ((contract[:1], contract[1:]), ((), ())), preferred_element_type=jnp.float32
    )


def projections(proj_ref, span):
    point_q, point_k = proj_ref[0, span], proj_ref[1, span]
    gate_q, gate_k = jax.nn.sigmoid(point_q), jax.nn.sigmoid(point_k)
    queries = (point_q * gate_q * HEAD_DIM ** (-0.5)).astype(jnp.bfloat16)
    keys = (point_k * gate_k).astype(jnp.bfloat16)
    values = proj_ref[2, span].astype(jnp.bfloat16)
    return (point_q, gate_q, queries), (point_k, gate_k, keys), values


def state_kernel(proj_ref, up_ref, start_ref, end_ref, key_ref, query_ref, total_ref):
    blocks = key_ref.shape[1]
    forward = jnp.zeros((HEAD_DIM, HEAD_DIM), jnp.float32)
    query_states, decays = [], []
    for b in range(blocks):
        span = pl.ds(b * BLOCK, BLOCK)
        (_, _, queries), (_, _, keys), values = projections(proj_ref, span)
        keys_weighted = (keys.astype(jnp.float32) * end_ref[0, span]).astype(jnp.bfloat16)
        queries_weighted = (queries.astype(jnp.float32) * start_ref[0, span]).astype(jnp.bfloat16)
        key_state = dot(keys_weighted, values, (0, 0))
        query_state = dot(queries_weighted, up_ref[span], (0, 0))
        key_ref[0, b] = key_state
        query_ref[0, b] = query_state
        decay = start_ref[0, pl.ds(b * BLOCK + BLOCK - 1, 1)]
        forward = decay * forward + key_state
        query_states.append(query_state)
        decays.append(decay)
    backward = jnp.zeros((HEAD_DIM, HEAD_DIM), jnp.float32)
    for b in reversed(range(blocks)):
        backward = decays[b] * backward + query_states[b]
    total_ref[0, 0] = forward.astype(jnp.bfloat16)
    total_ref[1, 0] = backward.astype(jnp.bfloat16)


def gradient_kernel(
    weight_ref, proj_ref, up_ref, start_ref, end_ref, pair_ref, key_ref, query_ref, *rest
):
    totals, out_ref = rest[:-1], rest[-1]
    blocks = key_ref.shape[1]
    head = pl.program_id(0)
    state = jnp.zeros((HEAD_DIM, HEAD_DIM), jnp.float32)
    reverse = jnp.zeros((HEAD_DIM, HEAD_DIM), jnp.float32)
    for k, total in enumerate(totals):
        state = state + weight_ref[0, k, head] * total[0, 0].astype(jnp.float32)
        reverse = reverse + weight_ref[1, k, head] * total[1, 0].astype(jnp.float32)
    decays = [start_ref[0, pl.ds(b * BLOCK + BLOCK - 1, 1)] for b in range(blocks)]
    after = [None] * blocks
    for b in reversed(range(blocks)):
        after[b] = reverse.astype(jnp.bfloat16)
        reverse = decays[b] * reverse + query_ref[0, b]
    for b in range(blocks):
        before = state.astype(jnp.bfloat16)
        state = decays[b] * state + key_ref[0, b]
        span = pl.ds(b * BLOCK, BLOCK)
        (point_q, gate_q, queries), (point_k, gate_k, keys), values = projections(proj_ref, span)
        upstream = up_ref[span]
        from_start, to_end, pair = start_ref[0, span], end_ref[0, span], pair_ref[0, b]
        query_key = (dot(queries, keys, (1, 1)) * pair).astype(jnp.bfloat16)
        value_score = (dot(upstream, values, (1, 1)) * pair).astype(jnp.bfloat16)
        query_gradient = dot(value_score, keys, (1, 0)) + from_start * dot(
            upstream, before, (1, 1)
        )
        key_gradient = dot(value_score, queries, (0, 0)) + to_end * dot(values, after[b], (1, 1))
        value_gradient = dot(query_key, upstream, (0, 0)) + to_end * dot(keys, after[b], (1, 0))
        slope_q = gate_q * (1.0 + point_q * (1.0 - gate_q)) * HEAD_DIM ** (-0.5)
        slope_k = gate_k * (1.0 + point_k * (1.0 - gate_k))
        out_ref[0, span] = (query_gradient * slope_q).astype(jnp.bfloat16)
        out_ref[1, span] = (key_gradient * slope_k).astype(jnp.bfloat16)
        out_ref[2, span] = value_gradient.astype(jnp.bfloat16)


def input_kernel(gradient_ref, weight_ref, out_ref):
    for first in range(0, out_ref.shape[0], BLOCK):
        span = pl.ds(first, BLOCK)
        total = dot(gradient_ref[0, span], weight_ref[0], (1, 1))
        for k in (1, 2):
            total = total + dot(gradient_ref[k, span], weight_ref[k], (1, 1))
        out_ref[span] = total.astype(jnp.bfloat16)


def body(inputs, projection, cotangent, log_decay, document_starts):
    tokens = inputs.shape[0]
    heads_here = log_decay.shape[0]
    local_cols = cotangent.shape[1]
    blocks = tokens // BLOCK
    features = lax.all_gather(inputs, "head", axis=1, tiled=True)
    rows = projection.shape[0]
    blocks_w = gather_rows(projection.transpose(1, 0, 2), "seq")

    def feature_rows(owner, first, count):
        return lax.dynamic_slice_in_dim(features, owner * rows + first, count, axis=1)

    offset = lax.axis_index("seq") * tokens
    positions = offset + jnp.arange(tokens, dtype=jnp.int32)
    doc_index = (
        jnp.sum((document_starts[None, :] <= positions[:, None]).astype(jnp.int32), axis=1) - 1
    )
    doc_begin = jnp.any(document_starts[None, :] == positions[:, None], axis=1).astype(jnp.int32)
    decay_sum = jnp.cumsum(log_decay.reshape(heads_here, blocks, BLOCK), axis=-1)
    pair_weight, to_end, from_start, block_decay = block_factors(
        decay_sum, doc_index.reshape(blocks, BLOCK), doc_begin.reshape(blocks, BLOCK)
    )
    lanes = (heads_here, tokens, HEAD_DIM)
    to_end = jnp.broadcast_to(to_end.reshape(heads_here, tokens)[..., None], lanes)
    from_start = jnp.broadcast_to(from_start.reshape(heads_here, tokens)[..., None], lanes)
    device_decay = jnp.prod(block_decay, axis=1)

    zero = jnp.zeros((), jnp.bfloat16)
    if len(blocks_w) > 2:
        owner, first, block = blocks_w[2]
        zero, block = lax.optimization_barrier((zero, block))
        blocks_w[2] = (owner, first, block)
    weights_all = jnp.broadcast_to(zero, (3, features.shape[1], local_cols))

    def place_rows(whole, some):
        for owner, first, block in some:
            whole = lax.dynamic_update_slice_in_dim(whole, block, owner * rows + first, axis=1)
        return whole

    early, late = blocks_w[:4], blocks_w[4:]
    weights_all = place_rows(weights_all, early)
    features, weights_all, from_start, to_end, pair_weight = lax.optimization_barrier(
        (features, weights_all, from_start, to_end, pair_weight)
    )
    projected = None
    for k, (owner, first, block) in enumerate(blocks_w):
        piece = jnp.einsum(
            "td,kdc->ktc",
            feature_rows(owner, first, block.shape[1]),
            block,
            preferred_element_type=jnp.float32,
        )
        projected = piece if projected is None else lax.optimization_barrier(projected) + piece
        if k == min(5, len(blocks_w) - 1):
            projected, device_decay = lax.optimization_barrier((projected, device_decay))
    weights_all = place_rows(weights_all, late)

    proj_spec = pl.BlockSpec((3, tokens, HEAD_DIM), lambda h: (0, 0, h))
    up_spec = pl.BlockSpec((tokens, HEAD_DIM), lambda h: (0, h))
    lane_spec = pl.BlockSpec((1, tokens, HEAD_DIM), lambda h: (h, 0, 0))
    state_spec = pl.BlockSpec((1, blocks, HEAD_DIM, HEAD_DIM), lambda h: (h, 0, 0, 0))
    total_spec = pl.BlockSpec((2, 1, HEAD_DIM, HEAD_DIM), lambda h: (0, h, 0, 0))
    pair_spec = pl.BlockSpec((1, blocks, BLOCK, BLOCK), lambda h: (h, 0, 0, 0))
    states = jax.ShapeDtypeStruct((heads_here, blocks, HEAD_DIM, HEAD_DIM), jnp.float32)
    key_state, query_state, totals = pl.pallas_call(
        state_kernel,
        grid=(heads_here,),
        in_specs=[proj_spec, up_spec, lane_spec, lane_spec],
        out_specs=[state_spec, state_spec, total_spec],
        out_shape=[
            states,
            states,
            jax.ShapeDtypeStruct((2, heads_here, HEAD_DIM, HEAD_DIM), jnp.bfloat16),
        ],
    )(projected, cotangent, from_start, to_end)
    parts, owners = gather_states(totals, "seq")
    weights = device_weights(device_decay, owners, "seq")
    project_gradient = pl.pallas_call(
        gradient_kernel,
        grid=(heads_here,),
        in_specs=[pl.BlockSpec(memory_space=pltpu.SMEM)]
        + [proj_spec, up_spec, lane_spec, lane_spec, pair_spec, state_spec, state_spec]
        + [total_spec] * len(parts),
        out_specs=proj_spec,
        out_shape=jax.ShapeDtypeStruct(projected.shape, jnp.bfloat16),
    )(weights, projected, cotangent, from_start, to_end, pair_weight, key_state, query_state, *parts)

    def weight_partial(gradient, owner, first, count):
        term = jnp.einsum(
            "td,ktc->kdc",
            feature_rows(owner, first, count),
            gradient,
            preferred_element_type=jnp.float32,
        ).astype(jnp.bfloat16)
        return with_layout_constraint(term, Layout(major_to_minor=(0, 1, 2)))

    def input_partial(gradient, part, of):
        columns = features.shape[1]
        tile, count = columns // 8, tokens // of
        return pl.pallas_call(
            input_kernel,
            grid=(columns // tile,),
            in_specs=[
                pl.BlockSpec((3, count, local_cols), lambda i: (0, part, 0)),
                pl.BlockSpec((3, tile, local_cols), lambda i: (0, i, 0)),
            ],
            out_specs=pl.BlockSpec((count, tile), lambda i: (0, i)),
            out_shape=jax.ShapeDtypeStruct((count, columns), jnp.bfloat16),
            cost_estimate=pl.CostEstimate(flops=1, bytes_accessed=1, transcendentals=0),
            compiler_params=pltpu.CompilerParams(vmem_limit_bytes=40 << 20),
        )(gradient, weights_all)

    input_partials, weight_gradient = scatter_rows(
        weight_partial, input_partial, project_gradient, "seq", rows
    )
    input_gradient = lax.psum_scatter(
        input_partials[0], "head", scatter_dimension=1, tiled=True
    )
    weight_gradient = weight_gradient.transpose(1, 0, 2)
    return (input_gradient, weight_gradient)


def solution(mesh):
    placed = (P("seq", "head"), P("seq", None, "head"), P("seq", "head"), P("head", "seq"), P())
    return jax.shard_map(
        body,
        mesh=mesh,
        in_specs=placed,
        out_specs=(P("seq", "head"), P("seq", None, "head")),
        check_vma=False,
    )
```
